32 devices in a mesh: groups: 2 (over y), rows: 4 (over z), tm: 4 (over x, core).
Axes of the slice: x: 2, y: 2, z: 4, core: 2. Of those that a mesh axis runs over, the one named last changes fastest.
Arguments:
- video: bfloat16 [2, 16, 8, 96, 128], P('groups', 'tm', 'rows'), parts along dimension 0, may hold values from -6 to 6
- gamma_first: float32 [96], replicated, may hold values from 0.25 to 1.75
- kernel_first: bfloat16 [96, 2592], replicated, may hold values from -0.125 to 0.125
- bias_first: float32 [96], replicated, may hold values from -3 to 3
- gamma_second: float32 [96], replicated, may hold values from 0.25 to 1.75
- kernel_second: bfloat16 [96, 2592], replicated, may hold values from -0.125 to 0.125
- bias_second: float32 [96], replicated, may hold values from -3 to 3
Outputs:
- encoded: bfloat16 [2, 16, 8, 96, 128], P('groups', 'tm', 'rows'), parts along dimension 0
The draws below stay inside these ranges and needn't reach their ends.
There are 2 independent parts, one for each index of `groups`. The reference program is written for one: setup_inputs(seed, part) draws one part's arguments, and reference() takes and returns one part's arrays. A program takes and returns all parts, laid end to end along the dimension named above; an argument that names none is the same for every part. Nothing has to cross between parts.
All inputs are finite; a program needn't handle non-finite values.
Results may differ from the reference program's by a relative error of at most 0.0036.
Values may be sent and summed in bfloat16 or wider, within the bound.
A program may use at most 64 MiB of HBM per device.

```python
import jax
import jax.numpy as jnp
from jax import lax

C = 96
CLIPS = 1
COLS = 128
FRAMES = 16
HEIGHT = 8


def steps_of(key, shape, split, smallest, largest):
    loudness, own = 1.0, jax.random.fold_in(key, 6)
    for dim, parts in split:
        steps = jnp.exp(jax.random.uniform(jax.random.fold_in(own, dim), (parts,), jnp.float32, smallest / len(split), largest / len(split)))
        loudness = loudness * jnp.repeat(steps, shape[dim] // parts).reshape([-1 if axis == dim else 1 for axis in range(len(shape))])
    return loudness


def normal_values(own_key, shape, scale, reach, pieces=(), kind=jnp.bfloat16):
    level = steps_of(own_key, shape, pieces, -0.22, 0.18) if pieces else 1.0
    entries = jax.random.normal(own_key, shape, jnp.float32) * scale * level
    return jnp.minimum(jnp.maximum(entries, -reach), reach).astype(kind)


def setup_inputs(seed: int = 0, part: int = 0) -> dict:
    seeds = jax.random.split(jax.random.key(seed), 8)
    part_splits = jax.random.split(jax.random.fold_in(seeds[7], part), 8)
    return {
        "video": normal_values(part_splits[0], (CLIPS, FRAMES, HEIGHT, C, COLS), 1.0, 6.0, ((1, 4), (2, 4))),
        "gamma_first": jnp.clip(1.0 + 0.15 * jax.random.normal(seeds[1], (C,), jnp.float32), 0.25, 1.75),
        "kernel_first": normal_values(seeds[2], (C, 27 * C), (27 * C) ** -0.5, 0.125),
        "bias_first": normal_values(seeds[3], (C,), 0.5, 3.0, (), jnp.float32),
        "gamma_second": jnp.clip(1.0 + 0.15 * jax.random.normal(seeds[4], (C,), jnp.float32), 0.25, 1.75),
        "kernel_second": normal_values(seeds[5], (C, 27 * C), (27 * C) ** -0.5, 0.125),
        "bias_second": normal_values(seeds[6], (C,), 0.5, 3.0, (), jnp.float32),
    }


epsilon = 1e-06

def norm_silu(values, gain):
    meansq = lax.optimization_barrier(jnp.mean(values * values, axis=3, keepdims=True))
    scaled = values * lax.rsqrt(meansq + epsilon) * gain[:, None]
    return jax.nn.silu(scaled)

def causal_conv(active, kernel, offset):
    clips, frames, height, chans, width = active.shape
    padded = jnp.pad(active, ((0, 0), (2, 0), (1, 1), (0, 0), (1, 1)))
    taps = kernel.astype(jnp.float32).reshape(chans, 3, 3, 3, chans)

    def one_frame(index):
        window = lax.dynamic_slice_in_dim(padded, index, 3, axis=1).astype(jnp.float32)
        summed = jnp.zeros((clips, height, chans, width), jnp.float32)
        for frame_off in range(3):
            for row_off in range(3):
                for col_off in range(3):
                    piece = window[:, frame_off, row_off:row_off + height, :, col_off:col_off + width]
                    summed = summed + jnp.einsum('oc,bhcw->bhow', taps[:, frame_off, row_off, col_off, :], piece, precision=lax.Precision.HIGHEST)
        return summed
    outputs = lax.map(one_frame, jnp.arange(frames, dtype=jnp.int32))
    return jnp.moveaxis(outputs, 0, 1) + offset[:, None]

def reference(video, gamma_first, kernel_first, bias_first, gamma_second, kernel_second, bias_second):
    first = norm_silu(video.astype(jnp.float32), gamma_first).astype(jnp.bfloat16)
    hidden = causal_conv(first, kernel_first, bias_first)
    second = norm_silu(hidden, gamma_second).astype(jnp.bfloat16)
    result = causal_conv(second, kernel_second, bias_second)
    return (video.astype(jnp.float32) + result).astype(jnp.bfloat16)
```

```python
import jax
import jax.numpy as jnp
from jax import lax
from jax.experimental import pallas as pl
from jax.experimental.pallas import tpu as pltpu
from jax.sharding import PartitionSpec as P

MESH = pl.DeviceIdType.MESH
epsilon = 1e-06


def block_kernel(
    video, k_first, k_second, g_first, b_first, g_second, b_second, out,
    ext_a, ext_b, st_a, st_b, w_a, w_b, vecs, local_sem, send_sem, recv_sem,
):
    frames, rows, chans, width = video.shape[1:]
    group = 9 * chans
    t = lax.axis_index("tm")
    r = lax.axis_index("rows")
    has_prev = t > 0
    has_next = t < lax.axis_size("tm") - 1
    has_up = r > 0
    has_down = r < lax.axis_size("rows") - 1

    def both(one, other):
        return jnp.logical_and(one, other)

    up, down = {"rows": r - 1}, {"rows": r + 1}
    later = {"tm": t + 1}
    later_up, later_down = {"tm": t + 1, "rows": r - 1}, {"tm": t + 1, "rows": r + 1}

    own = pltpu.make_async_copy(video.at[0], ext_a.at[2:, 1 : rows + 1], local_sem.at[0])
    load_a = pltpu.make_async_copy(k_first, w_a, local_sem.at[1])
    load_b = pltpu.make_async_copy(k_second, w_b, local_sem.at[2])
    own.start()
    load_a.start()
    load_b.start()

    barrier = pltpu.get_barrier_semaphore()
    prev, prev_up, prev_down = {"tm": t - 1}, {"tm": t - 1, "rows": r - 1}, {"tm": t - 1, "rows": r + 1}
    for cond, where in (
        (has_up, up), (has_down, down), (has_prev, prev),
        (both(has_prev, has_up), prev_up), (both(has_prev, has_down), prev_down),
    ):
        @pl.when(cond)
        def _():
            pl.semaphore_signal(barrier, inc=1, device_id=where, device_id_type=MESH)
    beside = has_up.astype(jnp.int32) + has_down.astype(jnp.int32)
    pl.semaphore_wait(barrier, beside + has_next.astype(jnp.int32) * (1 + beside))

    def copies(source, ext, first, last, slot, over_time):
        f = slice(first, last)
        e = slice(first + 2, last + 2)
        plan = [
            (source.at[f, 0], ext.at[e, rows + 1], up, has_up, has_down),
            (source.at[f, rows - 1], ext.at[e, 0], down, has_down, has_up),
        ]
        if over_time:
            h = slice(frames - 2, frames)
            z = slice(0, 2)
            plan += [
                (source.at[h, 0:rows], ext.at[z, 1 : rows + 1], later, has_next, has_prev),
                (source.at[h, 0], ext.at[z, rows + 1], later_up, both(has_next, has_up), both(has_prev, has_down)),
                (source.at[h, rows - 1], ext.at[z, 0], later_down, both(has_next, has_down), both(has_prev, has_up)),
            ]
        made = []
        for n, (src, dst, where, sends, takes) in enumerate(plan):
            copy = pltpu.make_async_remote_copy(
                src_ref=src, dst_ref=dst, send_sem=send_sem.at[slot + n], recv_sem=recv_sem.at[slot + n],
                device_id=where, device_id_type=MESH,
            )
            made.append((copy, sends, takes))
        return made

    def start(made):
        for copy, sends, _ in made:
            pl.when(sends)(copy.start)

    def taken(made):
        for copy, _, takes in made:
            pl.when(takes)(copy.wait_recv)

    def sent(made):
        for copy, sends, _ in made:
            pl.when(sends)(copy.wait_send)

    moved = copies(video.at[0], ext_a, 0, frames, 0, True)
    start(moved)

    for ext in (ext_a, ext_b):
        @pl.when(jnp.logical_not(has_up))
        def _():
            ext[:, 0] = jnp.zeros((frames + 2, chans, width), jnp.bfloat16)

        @pl.when(jnp.logical_not(has_down))
        def _():
            ext[:, rows + 1] = jnp.zeros((frames + 2, chans, width), jnp.bfloat16)

        @pl.when(jnp.logical_not(has_prev))
        def _():
            ext[0:2] = jnp.zeros((2, rows + 2, chans, width), jnp.bfloat16)

    for n, ref in enumerate((g_first, b_first, g_second, b_second)):
        vecs[n] = jnp.broadcast_to(ref[...], (width, chans)).T

    lane = lax.broadcasted_iota(jnp.int32, (chans, width), 1)

    def act(values, gain):
        meansq = jnp.sum(values * values, axis=0, keepdims=True) * (1.0 / chans)
        half = values * lax.rsqrt(meansq + epsilon) * (gain * 0.5)
        return half + half * jnp.tanh(half)

    def place(stack, f, p, field):
        shifted = [
            jnp.where(lane == 0, 0.0, pltpu.roll(field, 1, 1)).astype(jnp.bfloat16),
            field.astype(jnp.bfloat16),
            jnp.where(lane == width - 1, 0.0, pltpu.roll(field, width - 1, 1)).astype(jnp.bfloat16),
        ]
        for row in range(rows):
            j = p - row
            if 0 <= j < 3:
                for k in range(3):
                    at = f * group + (j * 3 + k) * chans
                    stack[at : at + chans, row * width : (row + 1) * width] = shifted[k]

    def first_at(f, p):
        place(st_a, f, p, act(ext_a[f, p].astype(jnp.float32), vecs[0]))

    def conv(weights, stack, f):
        return jnp.dot(
            weights[...], stack[f * group : (f + 3) * group, :], preferred_element_type=jnp.float32
        )

    def second_of(f):
        total = conv(w_a, st_a, f)
        for row in range(rows):
            value = act(total[:, row * width : (row + 1) * width] + vecs[1], vecs[2])
            ext_b[f + 2, row + 1] = value.astype(jnp.bfloat16)
            place(st_b, f + 2, row + 1, value)

    def encoded_of(f):
        total = conv(w_b, st_b, f)
        for row in range(rows):
            value = total[:, row * width : (row + 1) * width] + vecs[3]
            out[0, f, row] = (ext_a[f + 2, row + 1].astype(jnp.float32) + value).astype(jnp.bfloat16)

    own.wait()
    for f in range(2, frames + 2):
        for p in range(1, rows + 1):
            first_at(f, p)
    load_a.wait()
    taken(moved[:2])
    for f in range(2, frames + 2):
        for p in (0, rows + 1):
            first_at(f, p)
    for f in range(2, frames):
        second_of(f)
    send_late = copies(ext_b.at[2:, 1 : rows + 1], ext_b, 2, frames, 5, True)
    start(send_late)
    taken(moved[2:])
    for f in range(2):
        for p in range(rows + 2):
            first_at(f, p)
    for f in range(2):
        second_of(f)
    send_early = copies(ext_b.at[2:, 1 : rows + 1], ext_b, 0, 2, 10, False)
    start(send_early)
    load_b.wait()
    taken(send_late)
    for f in range(2):
        for p in range(rows + 2):
            place(st_b, f, p, ext_b[f, p].astype(jnp.float32))
    for f in range(4, frames + 2):
        for p in (0, rows + 1):
            place(st_b, f, p, ext_b[f, p].astype(jnp.float32))
    taken(send_early)
    for f in range(2, 4):
        for p in (0, rows + 1):
            place(st_b, f, p, ext_b[f, p].astype(jnp.float32))
    for f in range(frames):
        encoded_of(f)
    sent(moved)
    sent(send_late)
    sent(send_early)


def local(video, gamma_first, kernel_first, bias_first, gamma_second, kernel_second, bias_second):
    frames, rows, chans, width = video.shape[1:]
    ext = pltpu.VMEM((frames + 2, rows + 2, chans, width), jnp.bfloat16)
    stack = pltpu.VMEM(((frames + 2) * 9 * chans, rows * width), jnp.bfloat16)
    weights = pltpu.VMEM(kernel_first.shape, jnp.bfloat16)
    vmem = pl.BlockSpec(memory_space=pltpu.VMEM)
    hbm = pl.BlockSpec(memory_space=pl.ANY)
    return pl.pallas_call(
        block_kernel,
        out_shape=jax.ShapeDtypeStruct(video.shape, jnp.bfloat16),
        in_specs=[hbm] * 3 + [vmem] * 4,
        out_specs=vmem,
        scratch_shapes=[
            ext, ext, stack, stack, weights, weights,
            pltpu.VMEM((4, chans, width), jnp.float32),
            pltpu.SemaphoreType.DMA((3,)),
            pltpu.SemaphoreType.DMA((12,)),
            pltpu.SemaphoreType.DMA((12,)),
        ],
        compiler_params=pltpu.CompilerParams(collective_id=0, has_side_effects=True),
        name="residual_block",
    )(
        video, kernel_first, kernel_second, gamma_first[None, :], bias_first[None, :],
        gamma_second[None, :], bias_second[None, :],
    )


def solution(mesh):
    in_specs = (P("groups", "tm", "rows", None, None), P(), P(), P(), P(), P(), P())
    out_specs = P("groups", "tm", "rows", None, None)
    return jax.shard_map(local, mesh=mesh, in_specs=in_specs, out_specs=out_specs, check_vma=False)
```

```python
import jax
import jax.numpy as jnp
from jax import lax
from jax.experimental import pallas as pl
from jax.experimental.pallas import tpu as pltpu
from jax.sharding import PartitionSpec as P

MESH = pl.DeviceIdType.MESH
epsilon = 1e-06


def block_kernel(
    video, k_first, k_second, g_first, b_first, g_second, b_second, out,
    ext_a, ext_b, st_a, st_b, w_a, w_b, vecs, small_0, small_1, small_2, small_3, local_sem, send_sem, recv_sem,
):
    frames, rows, chans, width = video.shape[1:]
    group = 9 * chans
    t = lax.axis_index("tm")
    r = lax.axis_index("rows")
    has_prev = t > 0
    has_next = t < lax.axis_size("tm") - 1
    has_up = r > 0
    has_down = r < lax.axis_size("rows") - 1

    def both(one, other):
        return jnp.logical_and(one, other)

    up, down = {"rows": r - 1}, {"rows": r + 1}
    later = {"tm": t + 1}
    later_up, later_down = {"tm": t + 1, "rows": r - 1}, {"tm": t + 1, "rows": r + 1}

    barrier = pltpu.get_barrier_semaphore()
    prev, prev_up, prev_down = {"tm": t - 1}, {"tm": t - 1, "rows": r - 1}, {"tm": t - 1, "rows": r + 1}
    for cond, where in (
        (has_up, up), (has_down, down), (has_prev, prev),
        (both(has_prev, has_up), prev_up), (both(has_prev, has_down), prev_down),
    ):
        @pl.when(cond)
        def _():
            pl.semaphore_signal(barrier, inc=1, device_id=where, device_id_type=MESH)
    own = pltpu.make_async_copy(video.at[0], ext_a.at[2:, 1 : rows + 1], local_sem.at[0])
    load_a = pltpu.make_async_copy(k_first, w_a, local_sem.at[1])
    load_b = pltpu.make_async_copy(k_second, w_b, local_sem.at[2])
    own.start()
    small = [
        pltpu.make_async_copy(src, dst, local_sem.at[3 + n])
        for n, (src, dst) in enumerate(
            ((g_first, small_0), (b_first, small_1), (g_second, small_2), (b_second, small_3))
        )
    ]
    for copy in small:
        copy.start()
    load_a.start()
    load_b.start()

    own.wait()
    beside = has_up.astype(jnp.int32) + has_down.astype(jnp.int32)
    pl.semaphore_wait(barrier, beside + has_next.astype(jnp.int32) * (1 + beside))

    def copies(source, ext, first, last, slot, over_time):
        f = slice(first, last)
        e = slice(first + 2, last + 2)
        plan = [
            (source.at[f, 0], ext.at[e, rows + 1], up, has_up, has_down),
            (source.at[f, rows - 1], ext.at[e, 0], down, has_down, has_up),
        ]
        if over_time:
            h = slice(frames - 2, frames)
            z = slice(0, 2)
            plan += [
                (source.at[h, 0:rows], ext.at[z, 1 : rows + 1], later, has_next, has_prev),
                (source.at[h, 0], ext.at[z, rows + 1], later_up, both(has_next, has_up), both(has_prev, has_down)),
                (source.at[h, rows - 1], ext.at[z, 0], later_down, both(has_next, has_down), both(has_prev, has_up)),
            ]
        made = []
        for n, (src, dst, where, sends, takes) in enumerate(plan):
            copy = pltpu.make_async_remote_copy(
                src_ref=src, dst_ref=dst, send_sem=send_sem.at[slot + n], recv_sem=recv_sem.at[slot + n],
                device_id=where, device_id_type=MESH,
            )
            made.append((copy, sends, takes))
        return made

    def start(made):
        for copy, sends, _ in made:
            pl.when(sends)(copy.start)

    def taken(made):
        for copy, _, takes in made:
            pl.when(takes)(copy.wait_recv)

    def sent(made):
        for copy, sends, _ in made:
            pl.when(sends)(copy.wait_send)

    moved = copies(ext_a.at[2:, 1 : rows + 1], ext_a, 0, frames, 0, True)
    start(moved)

    for ext in (ext_a, ext_b):
        @pl.when(jnp.logical_not(has_up))
        def _():
            ext[:, 0] = jnp.zeros((frames + 2, chans, width), jnp.bfloat16)

        @pl.when(jnp.logical_not(has_down))
        def _():
            ext[:, rows + 1] = jnp.zeros((frames + 2, chans, width), jnp.bfloat16)

        @pl.when(jnp.logical_not(has_prev))
        def _():
            ext[0:2] = jnp.zeros((2, rows + 2, chans, width), jnp.bfloat16)

    for n, ref in enumerate((small_0, small_1, small_2, small_3)):
        small[n].wait()
        vecs[n] = jnp.broadcast_to(ref[...], (width, chans)).T

    lane = lax.broadcasted_iota(jnp.int32, (chans, width), 1)

    def act(values, gain):
        meansq = jnp.sum(values * values, axis=0, keepdims=True) * (1.0 / chans)
        half = values * lax.rsqrt(meansq + epsilon) * (gain * 0.5)
        return half + half * jnp.tanh(half)

    def place(stack, f, p, field):
        shifted = [
            jnp.where(lane == 0, 0.0, pltpu.roll(field, 1, 1)).astype(jnp.bfloat16),
            field.astype(jnp.bfloat16),
            jnp.where(lane == width - 1, 0.0, pltpu.roll(field, width - 1, 1)).astype(jnp.bfloat16),
        ]
        for row in range(rows):
            j = p - row
            if 0 <= j < 3:
                for k in range(3):
                    at = f * group + (j * 3 + k) * chans
                    stack[at : at + chans, row * width : (row + 1) * width] = shifted[k]

    def first_at(f, p):
        place(st_a, f, p, act(ext_a[f, p].astype(jnp.float32), vecs[0]))

    def conv(weights, stack, f):
        return jnp.dot(
            weights[...], stack[f * group : (f + 3) * group, :], preferred_element_type=jnp.float32
        )

    def second_of(f):
        total = conv(w_a, st_a, f)
        for row in range(rows):
            value = act(total[:, row * width : (row + 1) * width] + vecs[1], vecs[2])
            ext_b[f + 2, row + 1] = value.astype(jnp.bfloat16)
            place(st_b, f + 2, row + 1, value)

    def encoded_of(f):
        total = conv(w_b, st_b, f)
        for row in range(rows):
            value = total[:, row * width : (row + 1) * width] + vecs[3]
            out[0, f, row] = (ext_a[f + 2, row + 1].astype(jnp.float32) + value).astype(jnp.bfloat16)

    for f in range(2, frames + 2):
        for p in range(1, rows + 1):
            first_at(f, p)
    load_a.wait()
    taken(moved[:2])
    for f in range(2, frames + 2):
        for p in (0, rows + 1):
            first_at(f, p)
    for f in range(2, frames):
        second_of(f)
    send_late = copies(ext_b.at[2:, 1 : rows + 1], ext_b, 2, frames, 5, True)
    start(send_late)
    taken(moved[2:])
    for f in range(2):
        for p in range(rows + 2):
            first_at(f, p)
    for f in range(2):
        second_of(f)
    send_early = copies(ext_b.at[2:, 1 : rows + 1], ext_b, 0, 2, 10, False)
    start(send_early)
    load_b.wait()
    taken(send_late)
    for f in range(2):
        for p in range(rows + 2):
            place(st_b, f, p, ext_b[f, p].astype(jnp.float32))
    for f in range(4, frames + 2):
        for p in (0, rows + 1):
            place(st_b, f, p, ext_b[f, p].astype(jnp.float32))
    taken(send_early)
    for f in range(2, 4):
        for p in (0, rows + 1):
            place(st_b, f, p, ext_b[f, p].astype(jnp.float32))
    for f in range(frames):
        encoded_of(f)
    sent(moved)
    sent(send_late)
    sent(send_early)


def local(video, gamma_first, kernel_first, bias_first, gamma_second, kernel_second, bias_second):
    frames, rows, chans, width = video.shape[1:]
    ext = pltpu.VMEM((frames + 2, rows + 2, chans, width), jnp.bfloat16)
    stack = pltpu.VMEM(((frames + 2) * 9 * chans, rows * width), jnp.bfloat16)
    weights = pltpu.VMEM(kernel_first.shape, jnp.bfloat16)
    vmem = pl.BlockSpec(memory_space=pltpu.VMEM)
    hbm = pl.BlockSpec(memory_space=pl.ANY)
    return pl.pallas_call(
        block_kernel,
        out_shape=pltpu.VMEM(video.shape, jnp.bfloat16),
        in_specs=[hbm] * 7,
        out_specs=vmem,
        scratch_shapes=[
            ext, ext, stack, stack, weights, weights,
            pltpu.VMEM((4, chans, width), jnp.float32),
            *[pltpu.VMEM((1, chans), jnp.float32)] * 4,
            pltpu.SemaphoreType.DMA((7,)),
            pltpu.SemaphoreType.DMA((12,)),
            pltpu.SemaphoreType.DMA((12,)),
        ],
        compiler_params=pltpu.CompilerParams(collective_id=0, has_side_effects=True),
        name="residual_block",
    )(
        video, kernel_first, kernel_second, gamma_first[None, :], bias_first[None, :],
        gamma_second[None, :], bias_second[None, :],
    )


def solution(mesh):
    in_specs = (P("groups", "tm", "rows", None, None), P(), P(), P(), P(), P(), P())
    out_specs = P("groups", "tm", "rows", None, None)
    return jax.shard_map(local, mesh=mesh, in_specs=in_specs, out_specs=out_specs, check_vma=False)
```

```python
import jax
import jax.numpy as jnp
from jax import lax
from jax.experimental import pallas as pl
from jax.experimental.pallas import tpu as pltpu
from jax.sharding import PartitionSpec as P

MESH = pl.DeviceIdType.MESH
epsilon = 1e-06


def block_kernel(
    video, k_first, k_second, g_first, b_first, g_second, b_second, out,
    ext, st_a, st_b, w_a, w_b, by_a, by_b, sum_a, sum_b, vecs, small_0, small_1, small_2, small_3, local_sem, send_sem, recv_sem,
):
    frames, rows, chans, width = video.shape[1:]
    group = 9 * chans
    t = lax.axis_index("tm")
    r = lax.axis_index("rows")
    has_prev = t > 0
    has_next = t < lax.axis_size("tm") - 1
    has_up = r > 0
    has_down = r < lax.axis_size("rows") - 1

    def both(one, other):
        return jnp.logical_and(one, other)

    up, down, later = {"rows": r - 1}, {"rows": r + 1}, {"tm": t + 1}

    barrier = pltpu.get_barrier_semaphore()
    for cond, where in ((has_up, up), (has_down, down), (has_prev, {"tm": t - 1})):
        @pl.when(cond)
        def _():
            pl.semaphore_signal(barrier, inc=1, device_id=where, device_id_type=MESH)

    own_rows = slice(2, 2 + rows)
    above, below = slice(0, 2), slice(2 + rows, 4 + rows)
    own = pltpu.make_async_copy(video.at[0], ext.at[frames:, own_rows], local_sem.at[0])
    load_a = pltpu.make_async_copy(k_first, w_a, local_sem.at[1])
    load_b = pltpu.make_async_copy(k_second, w_b, local_sem.at[2])
    own.start()
    small = [
        pltpu.make_async_copy(src, dst, local_sem.at[3 + n])
        for n, (src, dst) in enumerate(
            ((g_first, small_0), (b_first, small_1), (g_second, small_2), (b_second, small_3))
        )
    ]
    for copy in small:
        copy.start()
    load_a.start()
    load_b.start()

    own.wait()
    pl.semaphore_wait(
        barrier, has_up.astype(jnp.int32) + has_down.astype(jnp.int32) + has_next.astype(jnp.int32)
    )

    order = list(range(frames))[::-1]

    def plan(slot, src, dst, where, sends, takes):
        copy = pltpu.make_async_remote_copy(
            src_ref=src, dst_ref=dst, send_sem=send_sem.at[slot], recv_sem=recv_sem.at[slot],
            device_id=where, device_id_type=MESH,
        )
        return copy, sends, takes

    beside, passed = {}, {}
    for f in range(frames):
        mine = ext.at[frames + f, own_rows]
        beside[f] = (
            plan(f, mine, ext.at[frames + f, below], up, has_up, has_down),
            plan(frames + f, mine, ext.at[frames + f, above], down, has_down, has_up),
        )
        passed[f] = (
            plan(2 * frames + f, ext.at[frames + f, below], ext.at[f, below], later,
                 both(has_next, has_down), both(has_prev, has_down)),
            plan(3 * frames + f, ext.at[frames + f, above], ext.at[f, above], later,
                 both(has_next, has_up), both(has_prev, has_up)),
        )
    onward = plan(4 * frames, ext.at[frames:, own_rows], ext.at[0:frames, own_rows], later, has_next, has_prev)

    def start(made):
        for copy, sends, _ in made:
            pl.when(sends)(copy.start)

    def taken(made):
        for copy, _, takes in made:
            pl.when(takes)(copy.wait_recv)

    def sent(made):
        for copy, sends, _ in made:
            pl.when(sends)(copy.wait_send)

    start(beside[order[0]])
    start([onward])
    for f in order[1:]:
        start(beside[f])

    @pl.when(jnp.logical_not(has_up))
    def _():
        ext[:, above] = jnp.zeros((2 * frames, 2, chans, width), jnp.bfloat16)

    @pl.when(jnp.logical_not(has_down))
    def _():
        ext[:, below] = jnp.zeros((2 * frames, 2, chans, width), jnp.bfloat16)

    @pl.when(jnp.logical_not(has_prev))
    def _():
        ext[0:frames] = jnp.zeros((frames, rows + 4, chans, width), jnp.bfloat16)

    for n, ref in enumerate((small_0, small_1, small_2, small_3)):
        small[n].wait()
        vecs[n] = jnp.broadcast_to(ref[...], (width, chans)).T

    lane = lax.broadcasted_iota(jnp.int32, (chans, width), 1)

    def act(values, gain):
        meansq = jnp.sum(values * values, axis=0, keepdims=True) * (1.0 / chans)
        half = values * lax.rsqrt(meansq + epsilon) * (gain * 0.5)
        return half + half * jnp.tanh(half)

    def place(stack, many, f, p, field):
        shifted = [
            jnp.where(lane == 0, 0.0, pltpu.roll(field, 1, 1)).astype(jnp.bfloat16),
            field.astype(jnp.bfloat16),
            jnp.where(lane == width - 1, 0.0, pltpu.roll(field, width - 1, 1)).astype(jnp.bfloat16),
        ]
        for row in range(many):
            j = p - row
            if 0 <= j < 3:
                for k in range(3):
                    at = f * group + (j * 3 + k) * chans
                    stack[at : at + chans, row * width : (row + 1) * width] = shifted[k]

    def first_at(f, places):
        for p in places:
            place(st_a, rows + 2, f, p, act(ext[f, p].astype(jnp.float32), vecs[0]))

    def split(weights, by_frame):
        for i in range(3):
            by_frame[i * chans : (i + 1) * chans, :] = weights[:, i * group : (i + 1) * group]

    def conv_step(by_frame, stack, sums, count, g):
        low, high = max(0, g - count + 1), min(2, g)
        total = jnp.dot(
            by_frame[low * chans : (high + 1) * chans, :], stack[g * group : (g + 1) * group, :],
            preferred_element_type=jnp.float32,
        )
        whole = None
        for i in range(low, high + 1):
            part = total[(i - low) * chans : (i - low + 1) * chans]
            if i == 2:
                sums[g - i] = part
            elif i == 1:
                sums[g - i] += part
            else:
                whole = sums[g] + part
        return whole

    one = jnp.float32(1.0)
    inside_up = jnp.where(has_up, one, 0.0)
    inside_down = jnp.where(has_down, one, 0.0)
    inside_prev = jnp.where(has_prev, one, 0.0)

    def step(g):
        total = conv_step(by_a, st_a, sum_a, frames + 2, g)
        if total is None:
            return
        for row in range(rows + 2):
            value = act(total[:, row * width : (row + 1) * width] + vecs[1], vecs[2])
            if row == 0:
                value = value * inside_up
            if row == rows + 1:
                value = value * inside_down
            if g < 2:
                value = value * inside_prev
            place(st_b, rows, g, row, value)
        total = conv_step(by_b, st_b, sum_b, frames, g)
        if total is None:
            return
        for row in range(rows):
            value = total[:, row * width : (row + 1) * width] + vecs[3]
            out[0, g, row] = (ext[frames + g, row + 2].astype(jnp.float32) + value).astype(jnp.bfloat16)

    middle = range(2, 2 + rows)
    edges = [0, 1, 2 + rows, 3 + rows]
    for f in order:
        first_at(frames + f, middle)
    load_a.wait()
    split(w_a, by_a)
    load_b.wait()
    split(w_b, by_b)
    for f in order:
        taken(beside[f])
        start(passed[f])
        first_at(frames + f, edges)
        step(frames + f)
    taken([onward])
    for f in order:
        first_at(f, middle)
    for f in order:
        taken(passed[f])
        first_at(f, edges)
        step(f)
    for f in order:
        sent(beside[f])
        sent(passed[f])
    sent([onward])


def local(video, gamma_first, kernel_first, bias_first, gamma_second, kernel_second, bias_second):
    frames, rows, chans, width = video.shape[1:]
    ext = pltpu.VMEM((2 * frames, rows + 4, chans, width), jnp.bfloat16)
    wide = pltpu.VMEM((2 * frames * 9 * chans, (rows + 2) * width), jnp.bfloat16)
    stack = pltpu.VMEM(((frames + 2) * 9 * chans, rows * width), jnp.bfloat16)
    weights = pltpu.VMEM(kernel_first.shape, jnp.bfloat16)
    by_frame = pltpu.VMEM((3 * chans, 9 * chans), jnp.bfloat16)
    vmem = pl.BlockSpec(memory_space=pltpu.VMEM)
    hbm = pl.BlockSpec(memory_space=pl.ANY)
    return pl.pallas_call(
        block_kernel,
        out_shape=pltpu.VMEM(video.shape, jnp.bfloat16),
        in_specs=[hbm] * 7,
        out_specs=vmem,
        scratch_shapes=[
            ext, wide, stack, weights, weights, by_frame, by_frame,
            pltpu.VMEM((frames + 2, chans, (rows + 2) * width), jnp.float32),
            pltpu.VMEM((frames, chans, rows * width), jnp.float32),
            pltpu.VMEM((4, chans, width), jnp.float32),
            *[pltpu.VMEM((1, chans), jnp.float32)] * 4,
            pltpu.SemaphoreType.DMA((7,)),
            pltpu.SemaphoreType.DMA((4 * frames + 1,)),
            pltpu.SemaphoreType.DMA((4 * frames + 1,)),
        ],
        compiler_params=pltpu.CompilerParams(collective_id=0, has_side_effects=True),
        name="residual_block",
    )(
        video, kernel_first, kernel_second, gamma_first[None, :], bias_first[None, :],
        gamma_second[None, :], bias_second[None, :],
    )


def solution(mesh):
    in_specs = (P("groups", "tm", "rows", None, None), P(), P(), P(), P(), P(), P())
    out_specs = P("groups", "tm", "rows", None, None)
    return jax.shard_map(local, mesh=mesh, in_specs=in_specs, out_specs=out_specs, check_vma=False)
```
